32 devices in a mesh: groups: 2 (over x), width: 8 (over z, y), guide: 2 (over core).
Axes of the slice: x: 2, y: 2, z: 4, core: 2. Of those that a mesh axis runs over, the one named last changes fastest.
Arguments:
- latent: float32 [16, 8, 2048], P(None, None, ('groups', 'width')), parts along dimension 2, may hold values from -6 to 6
- starts: int32 [16], P(('groups', 'width')), parts along dimension 0, may hold values from 0 to 1023, as said below
- counts: int32 [2048], P(('groups', 'width')), parts along dimension 0, may hold values from 1 to 3, as said below
- step_index: int32 [2], P('groups'), parts along dimension 0, may hold values from 0 to 27
- cond_mod: float32 [2, 3, 2432], P('guide'), may hold values from -3 to 3
- w_patch: bfloat16 [64, 2432], replicated, may hold values from -0.75 to 0.75
- w_qkv: bfloat16 [2432, 3840], P('width'), may hold values from -0.125 to 0.125
- w_out: bfloat16 [1280, 2432], replicated, may hold values from -0.15625 to 0.15625
- w_final: bfloat16 [2432, 64], replicated, may hold values from -0.125 to 0.125
- w_dec: bfloat16 [144, 512], replicated, may hold values from -0.5 to 0.5
Outputs:
- denoised: float32 [16, 8, 2048], P(None, 'guide', ('groups', 'width')), parts along dimension 2
- features: bfloat16 [8, 2048, 512], P('guide', ('groups', 'width')), parts along dimension 1
The draws below stay inside these ranges and needn't reach their ends.
There are 2 independent parts, one for each index of `groups`. The reference program is written for one: setup_inputs(seed, part) draws one part's arguments, and reference() takes and returns one part's arrays. A program takes and returns all parts, laid end to end along the dimension named above; an argument that names none is the same for every part. Nothing has to cross between parts.
Inputs may be any that keep to these rules, and one draw needn't show every extreme that they name: window k starts between column k * 128 and column (k + 1) * 128 - 1 and covers 2 * 128 columns, wrapping around the panorama. `counts`: the number of windows whose columns, as given by starts, include the column.
All inputs are finite; a program needn't handle non-finite values.
Results may differ from the reference program's by a relative error of at most 0.013.
Values may be sent and summed in bfloat16 or wider, within the bound.
A program may use at most 128 MiB of HBM per device.

```python
import jax
import jax.numpy as jnp
from jax import lax

D = 2432
HEADS = 20
HEAD = 64
LAT = 16
DEC = 512
STEPS = 28
HL = 8
COLS = 128
WL = 1024
NWIN = 8


def window_begins(key):
    offsets = jax.random.randint(jax.random.fold_in(key, 11), (NWIN,), 0, COLS, dtype=jnp.int32)
    return jnp.arange(NWIN, dtype=jnp.int32) * COLS + offsets


def draw_starts(key, part):
    return window_begins(key)


def draw_counts(key, part):
    begins = window_begins(key)
    columns = jnp.arange(WL, dtype=jnp.int32)
    covered = (columns[None, :] - begins[:, None]) % WL < 2 * COLS
    return jnp.sum(covered.astype(jnp.int32), axis=0).astype(jnp.int32)


def shard_levels(key, shape, shards, low, largest):
    def one(position, blocks):
        heights = jax.random.uniform(jax.random.fold_in(jax.random.fold_in(key, 6), position), (blocks,), jnp.float32, low / len(shards), largest / len(shards))
        return jnp.repeat(jnp.exp(heights), shape[position] // blocks).reshape((-1,) + (1,) * (len(shape) - position - 1))

    gain = one(*shards[0])
    for cut in shards[1:]:
        gain = gain * one(*cut)
    return gain


def gaussian(own_key, shape, scale, most, pieces=(), kind=jnp.bfloat16):
    values = scale * jax.random.normal(own_key, shape, jnp.float32)
    if pieces:
        values = values * shard_levels(own_key, shape, pieces, -0.22, 0.18)
    return jnp.clip(values, -most, most).astype(kind)


def setup_inputs(seed: int = 0, part: int = 0) -> dict:
    arg_keys = jax.random.split(jax.random.key(seed), 11)
    part_splits = jax.random.split(jax.random.fold_in(arg_keys[10], part), 11)
    return {
        "latent": gaussian(part_splits[0], (LAT, HL, WL), 1.0, 6.0, ((2, 8),), jnp.float32),
        "starts": draw_starts(jax.random.fold_in(jax.random.fold_in(arg_keys[10], part), 71), part),
        "counts": draw_counts(jax.random.fold_in(jax.random.fold_in(arg_keys[10], part), 71), part),
        "step_index": jax.random.randint(part_splits[3], (1,), 0, STEPS).astype(jnp.int32),
        "cond_mod": gaussian(arg_keys[4], (2, 3, D), 0.5, 3.0, ((0, 2),), jnp.float32),
        "w_patch": gaussian(arg_keys[5], (4 * LAT, D), (4 * LAT) ** -0.5, 0.75),
        "w_qkv": gaussian(arg_keys[6], (D, 3 * HEADS * HEAD), D ** -0.5, 0.125, ((0, 8),)),
        "w_out": gaussian(arg_keys[7], (HEADS * HEAD, D), (HEADS * HEAD) ** -0.5, 0.15625),
        "w_final": gaussian(arg_keys[8], (D, 4 * LAT), D ** -0.5, 0.125),
        "w_dec": gaussian(arg_keys[9], (9 * LAT, DEC), (9 * LAT) ** -0.5, 0.5),
    }


guidance = 4.0
epsilon = 1e-06

def layer_norm(values):
    centered = values - lax.optimization_barrier(jnp.mean(values, axis=-1, keepdims=True))
    spread = lax.optimization_barrier(jnp.mean(centered * centered, axis=-1, keepdims=True))
    return centered * lax.rsqrt(spread + epsilon)

def head_norm(values):
    return values * lax.rsqrt(lax.optimization_barrier(jnp.mean(values * values, axis=-1, keepdims=True)) + epsilon)

def patchify(window):
    channels, height, breadth = window.shape
    folded = window.reshape(channels, height // 2, 2, breadth // 2, 2).transpose(1, 3, 2, 4, 0)
    return folded.reshape(height // 2 * (breadth // 2), 4 * channels)

def unpatchify(tokens, channels, height, breadth):
    folded = tokens.reshape(height // 2, breadth // 2, 2, 2, channels).transpose(4, 0, 2, 1, 3)
    return folded.reshape(channels, height, breadth)

def attend(queries, key_rows, value_rows):
    scores = jnp.einsum('bqhe,bkhe->bhqk', queries.astype(jnp.float32), key_rows.astype(jnp.float32))
    scores = scores / jnp.sqrt(jnp.float32(queries.shape[-1]))
    weights = jax.nn.softmax(scores, axis=-1).astype(jnp.bfloat16)
    mixed = jnp.einsum('bhqk,bkhe->bqhe', weights.astype(jnp.float32), value_rows.astype(jnp.float32))
    return mixed.astype(jnp.bfloat16)

def convolve(padded, w_dec):
    channels = padded.shape[0]
    height = padded.shape[1] - 2
    breadth = padded.shape[2] - 2
    shifted = [padded[:, row_at:row_at + height, col_at:col_at + breadth] for row_at in range(3) for col_at in range(3)]
    stacked = jnp.stack(shifted).reshape(9 * channels, height * breadth)
    summed = lax.dot_general(stacked, w_dec, (((0,), (0,)), ((), ())), preferred_element_type=jnp.float32)
    return jax.nn.silu(summed).astype(jnp.bfloat16).reshape(height, breadth, w_dec.shape[1])

def branch_velocity(window, modulation, w_patch, w_qkv, w_out, w_final):
    patches = patchify(window)
    token_count = patches.shape[0]
    hidden = jnp.dot(patches, w_patch, preferred_element_type=jnp.float32)
    modulated = (layer_norm(hidden) * (1.0 + modulation[1]) + modulation[0]).astype(jnp.bfloat16)
    projected = jnp.dot(modulated, w_qkv, preferred_element_type=jnp.float32).reshape(token_count, 3, HEADS, HEAD)
    queries = head_norm(projected[:, 0]).astype(jnp.bfloat16)
    key_rows = head_norm(projected[:, 1]).astype(jnp.bfloat16)
    value_rows = projected[:, 2].astype(jnp.bfloat16)
    attended = attend(queries[None], key_rows[None], value_rows[None])[0].reshape(token_count, HEADS * HEAD)
    residual = hidden + modulation[2] * jnp.dot(attended, w_out, preferred_element_type=jnp.float32)
    final_in = layer_norm(residual).astype(jnp.bfloat16)
    result = jnp.dot(final_in, w_final, preferred_element_type=jnp.float32)
    return unpatchify(result, window.shape[0], window.shape[1], window.shape[2])

def reference(latent, starts, counts, step_index, cond_mod, w_patch, w_qkv, w_out, w_final, w_dec):
    fraction = (step_index[0].astype(jnp.float32) + 1.0) / STEPS
    sigma = 3.0 * fraction / (1.0 + 2.0 * fraction)
    total_cols = latent.shape[2]
    rounded = latent.astype(jnp.bfloat16)

    def one_window(summed, begin):
        columns_at = ((begin + jnp.arange(2 * COLS, dtype=jnp.int32)) % total_cols).astype(jnp.int32)
        window = jnp.take(rounded, columns_at, axis=2)
        conditional = branch_velocity(window, cond_mod[0], w_patch, w_qkv, w_out, w_final)
        plain = branch_velocity(window, cond_mod[1], w_patch, w_qkv, w_out, w_final)
        guided = plain + guidance * (conditional - plain)
        return (summed.at[:, :, columns_at].add(guided), None)
    summed, unused = lax.scan(one_window, jnp.zeros(latent.shape, jnp.float32), starts)
    velocity = summed / counts.astype(jnp.float32)[None, None, :]
    denoised = latent - sigma * velocity
    padded = jnp.pad(denoised.astype(jnp.bfloat16), ((0, 0), (1, 1), (1, 1)))
    features = convolve(padded, w_dec)
    return (denoised, features)
```

```python
import jax
import jax.numpy as jnp
from jax import lax
from jax.sharding import PartitionSpec as P

HEAD = 64
STEPS = 28


guidance = 4.0
epsilon = 1e-06


def from_behind(x, axis, by):
    peers = lax.axis_size(axis)
    return lax.ppermute(x, axis, [(i, (i + by) % peers) for i in range(peers)])


def from_partner(block, axis, stride):
    count = lax.axis_size(axis)
    route = []
    for low in range(count):
        high = low | 1 << stride
        if high != low and high < count:
            route += [(low, high), (high, low)]
    return lax.ppermute(block, axis, route)


def extended(block, sides, width):
    for axis, dim in sides:
        count = lax.axis_size(axis)
        forward = [(i, i + 1) for i in range(count - 1)]
        backward = [(target, source) for source, target in forward]
        low = lax.ppermute(
            lax.slice_in_dim(block, block.shape[dim] - width, None, axis=dim), axis, forward
        )
        high = lax.ppermute(lax.slice_in_dim(block, 0, width, axis=dim), axis, backward)
        block = jnp.concatenate([low, block, high], axis=dim)
    return block


def layer_norm(values):
    centered = values - jnp.mean(values, axis=-1, keepdims=True)
    spread = jnp.mean(centered * centered, axis=-1, keepdims=True)
    return centered * lax.rsqrt(spread + epsilon)


def head_norm(values):
    return values * lax.rsqrt(jnp.mean(values * values, axis=-1, keepdims=True) + epsilon)


def patchify(window):
    channels, height, breadth = window.shape
    folded = window.reshape(channels, height // 2, 2, breadth // 2, 2).transpose(1, 3, 2, 4, 0)
    return folded.reshape(height // 2 * (breadth // 2), 4 * channels)


def unpatchify(tokens, channels, height, breadth):
    folded = tokens.reshape(height // 2, breadth // 2, 2, 2, channels).transpose(4, 0, 2, 1, 3)
    return folded.reshape(channels, height, breadth)


def attend(queries, key_rows, value_rows):
    scores = jnp.einsum("bqhe,bkhe->bhqk", queries, key_rows, preferred_element_type=jnp.float32)
    scores = scores / jnp.sqrt(jnp.float32(queries.shape[-1]))
    weights = jax.nn.softmax(scores, axis=-1).astype(jnp.bfloat16)
    mixed = jnp.einsum("bhqk,bkhe->bqhe", weights, value_rows, preferred_element_type=jnp.float32)
    return mixed.astype(jnp.bfloat16)


def convolve(padded, w_dec):
    channels = padded.shape[0]
    height = padded.shape[1] - 2
    breadth = padded.shape[2] - 2
    shifted = [
        padded[:, row_at : row_at + height, col_at : col_at + breadth]
        for row_at in range(3)
        for col_at in range(3)
    ]
    stacked = jnp.stack(shifted).reshape(9 * channels, height * breadth)
    summed = lax.dot_general(
        stacked, w_dec, (((0,), (0,)), ((), ())), preferred_element_type=jnp.float32
    )
    return jax.nn.silu(summed).astype(jnp.bfloat16).reshape(height, breadth, w_dec.shape[1])


def halves(values):
    high = lax.reduce_precision(values, 8, 7)
    return high.astype(jnp.bfloat16), (values - high).astype(jnp.bfloat16)


def fold(modulation, w_patch, w_qkv, place):
    patch = w_patch.astype(jnp.float32)
    patch = patch - jnp.mean(patch, axis=1, keepdims=True)
    rows = jnp.concatenate([patch * (1.0 + modulation[1]), modulation[0:1]], axis=0)
    depth = w_qkv.shape[0]
    rows = lax.dynamic_slice_in_dim(rows, place * depth, depth, 1)
    high, low = halves(rows)
    both = jnp.dot(
        jnp.concatenate([high, low], axis=0), w_qkv, preferred_element_type=jnp.float32
    )
    return both[: rows.shape[0]] + both[rows.shape[0] :]


def fetch_next(block):
    return from_behind(block, "width", -1)


def pass_right(block):
    return from_behind(block.astype(jnp.bfloat16), "width", 1).astype(block.dtype)


def shards(latent, starts, counts, step_index, cond_mod, w_patch, w_qkv, w_out, w_final, w_dec):
    guide_at = lax.axis_index("guide")
    place = lax.axis_index("width")
    channels, height, columns = latent.shape
    half_rows = height // 2
    fraction = (step_index[0].astype(jnp.float32) + 1.0) / STEPS
    sigma = 3.0 * fraction / (1.0 + 2.0 * fraction)
    modulation = cond_mod[0]
    own_cols = latent.astype(jnp.bfloat16)
    ahead = fetch_next(own_cols)
    further = fetch_next(ahead)
    three_blocks = jnp.concatenate([own_cols, ahead, further], axis=2)
    offset = starts[0] - place * columns
    window = lax.dynamic_slice_in_dim(three_blocks, offset, 2 * columns, 2)
    patches = patchify(window)
    token_count = patches.shape[0]
    hidden = jnp.dot(patches, w_patch, preferred_element_type=jnp.float32)
    centered = hidden - jnp.mean(hidden, axis=-1, keepdims=True)
    rstd = lax.rsqrt(jnp.mean(centered * centered, axis=-1, keepdims=True) + epsilon)
    heads = w_qkv.shape[1] // (3 * HEAD)
    folded = lax.psum(fold(modulation, w_patch, w_qkv, place), "width")
    patch_rows = w_patch.shape[0]
    high, low = halves(folded[:patch_rows])
    projected = jnp.dot(
        jnp.concatenate([patches, patches], axis=1),
        jnp.concatenate([high, low], axis=0),
        preferred_element_type=jnp.float32,
    )
    projected = projected * rstd + folded[patch_rows : patch_rows + 1]
    projected = projected.reshape(token_count, 3, heads, HEAD)
    queries = head_norm(projected[:, 0]).astype(jnp.bfloat16)
    key_rows = head_norm(projected[:, 1]).astype(jnp.bfloat16)
    value_rows = projected[:, 2].astype(jnp.bfloat16)
    attended = attend(queries[None], key_rows[None], value_rows[None])[0]
    attended = attended.reshape(token_count, heads * HEAD)
    mixed_out = jnp.dot(attended, w_out, preferred_element_type=jnp.float32)
    residual = hidden + modulation[2] * mixed_out
    final_in = layer_norm(residual).astype(jnp.bfloat16)
    result = jnp.dot(final_in, w_final, preferred_element_type=jnp.float32)
    velocity_win = unpatchify(result, channels, height, 2 * columns)
    branch_pair = lax.all_to_all(
        velocity_win[None].astype(jnp.bfloat16), "guide", split_axis=2, concat_axis=0, tiled=True
    ).astype(jnp.float32)
    guided = branch_pair[1] + guidance * (branch_pair[0] - branch_pair[1])
    spread_out = jnp.zeros((channels, half_rows, 3 * columns), jnp.float32)
    spread_out = lax.dynamic_update_slice_in_dim(spread_out, guided, offset, 2)
    carried = pass_right(spread_out[:, :, 2 * columns :])
    arrived = pass_right(spread_out[:, :, columns : 2 * columns] + carried)
    summed = spread_out[:, :, :columns] + arrived
    velocity = summed / counts.astype(jnp.float32)[None, None, :]
    mine_rows = lax.dynamic_slice_in_dim(latent, guide_at * half_rows, half_rows, 1)
    denoised = mine_rows - sigma * velocity
    padded = extended(denoised.astype(jnp.bfloat16), (("guide", 1), ("width", 2)), 1)
    features = convolve(padded, w_dec)
    return (denoised, features)


def solution(mesh):
    return jax.shard_map(
        shards,
        mesh=mesh,
        in_specs=(
            P(None, None, ("groups", "width")),
            P(("groups", "width")),
            P(("groups", "width")),
            P("groups"),
            P("guide", None, None),
            P(),
            P("width", None),
            P(),
            P(),
            P(),
        ),
        out_specs=(P(None, "guide", ("groups", "width")), P("guide", ("groups", "width"), None)),
        check_vma=False,
    )
```

```python
import functools
import math

import jax
import jax.numpy as jnp
from jax import lax
from jax.experimental import pallas as pl
from jax.experimental.pallas import tpu as pltpu
from jax.sharding import PartitionSpec as P

HEAD = 64
STEPS = 28
LANES = 128
MESH = pl.DeviceIdType.MESH

guidance = 4.0
epsilon = 1e-06


def halves(values):
    high = lax.reduce_precision(values, 8, 7)
    return high.astype(jnp.bfloat16), (values - high).astype(jnp.bfloat16)


def fold_rows(modulation, w_patch, depth, place):
    patch = w_patch.astype(jnp.float32)
    means = jnp.mean(patch, axis=1, keepdims=True)
    part = lax.dynamic_slice_in_dim(w_patch, place * depth, depth, 1).astype(jnp.float32)
    mod = lax.dynamic_slice_in_dim(modulation, place * depth, depth, 1)
    rows = jnp.concatenate([(part - means) * (1.0 + mod[1]), mod[0:1]], axis=0)
    spare = -rows.shape[0] % 16
    rows = jnp.pad(rows, ((0, spare), (0, 0)))
    return jnp.concatenate(halves(rows), axis=0)


def at(groups, width):
    return {"groups": groups, "width": width}


def gather_kernel(
    groups, n, last, lhs, w_qkv, aux, full, auxs,
    own, parts, arrived, send_a, recv_a, send_b, recv_b, send_x, recv_x,
):
    g = lax.axis_index("groups")
    w = lax.axis_index("width")
    owners = groups * n
    me = g * n + w
    rows, size = full.shape[1:]
    barrier = pltpu.get_barrier_semaphore()

    @pl.loop(1, owners)
    def _(step):
        to = lax.rem(me + step, owners)
        pl.semaphore_signal(
            barrier, inc=1, device_id=at(to // n, lax.rem(to, n)), device_id_type=MESH
        )

    def piece(to):
        chunk = jnp.minimum(g * n + to, last)
        columns = pl.ds(pl.multiple_of(chunk * size, LANES), size)
        both = jnp.dot(lhs[...], w_qkv[:, columns], preferred_element_type=jnp.float32)
        return both[:rows] + both[rows:]

    @pl.loop(1, n)
    def _(step):
        parts[step] = piece(lax.rem(w + step, n)).astype(jnp.bfloat16)

    own[...] = piece(w)
    pl.semaphore_wait(barrier, owners - 1)

    def across(slot, shift):
        return pltpu.make_async_remote_copy(
            src_ref=aux, dst_ref=auxs.at[slot],
            send_sem=send_x.at[slot], recv_sem=recv_x.at[slot],
            device_id=at(g, lax.rem(w + shift + n, n)), device_id_type=MESH,
        )

    def scatter(step):
        return pltpu.make_async_remote_copy(
            src_ref=parts.at[step], dst_ref=arrived.at[step],
            send_sem=send_a.at[step], recv_sem=recv_a.at[step],
            device_id=at(g, lax.rem(w + step, n)), device_id_type=MESH,
        )

    @pl.loop(1, n)
    def _(step):
        scatter(step).start()

    moves = [across(0, -1), across(1, -2), across(2, 1)]
    for move in moves:
        move.start()

    @pl.loop(1, n)
    def _(step):
        scatter(step).wait_recv()

    def add(step, total):
        return total + arrived[step].astype(jnp.float32)

    full[me] = lax.fori_loop(1, n, add, own[...]).astype(jnp.bfloat16)

    def share(step):
        to = lax.rem(me + step, owners)
        return pltpu.make_async_remote_copy(
            src_ref=full.at[me], dst_ref=full.at[me],
            send_sem=send_b.at[step], recv_sem=recv_b.at[step],
            device_id=at(to // n, lax.rem(to, n)), device_id_type=MESH,
        )

    def shared(step):
        source = lax.rem(me - step + owners, owners)
        return pltpu.make_async_remote_copy(
            src_ref=full.at[source], dst_ref=full.at[source],
            send_sem=send_b.at[step], recv_sem=recv_b.at[step],
            device_id=at(source // n, lax.rem(source, n)), device_id_type=MESH,
        )

    @pl.loop(1, owners)
    def _(step):
        share(step).start()

    @pl.loop(1, owners)
    def _(step):
        shared(step).wait_recv()

    @pl.loop(1, n)
    def _(step):
        scatter(step).wait_send()

    @pl.loop(1, owners)
    def _(step):
        share(step).wait_send()

    for move in moves:
        move.wait()


def gather_folded(groups, n, lhs, w_qkv, aux):
    columns = w_qkv.shape[1]
    owners = groups * n
    third = columns // 3
    size = LANES * -(-columns // (LANES * owners))
    while third % size:
        size += LANES
    rows = lhs.shape[0] // 2
    dma = pltpu.SemaphoreType.DMA
    vmem = pl.BlockSpec(memory_space=pltpu.VMEM)
    return pl.pallas_call(
        functools.partial(gather_kernel, groups, n, columns // size - 1),
        name="gather_folded",
        out_shape=(
            jax.ShapeDtypeStruct((owners, rows, size), jnp.bfloat16),
            jax.ShapeDtypeStruct((3, *aux.shape), aux.dtype),
        ),
        in_specs=[vmem] * 3,
        out_specs=(vmem, vmem),
        scratch_shapes=[
            pltpu.VMEM((rows, size), jnp.float32),
            pltpu.VMEM((n, rows, size), jnp.bfloat16),
            pltpu.VMEM((n, rows, size), jnp.bfloat16),
            dma((n,)), dma((n,)), dma((owners,)), dma((owners,)), dma((3,)), dma((3,)),
        ],
        compiler_params=pltpu.CompilerParams(
            collective_id=0, has_side_effects=True, vmem_limit_bytes=32 << 20
        ),
    )(lhs, w_qkv, aux)


def column_map(shape, column_dim, parity, offset):
    column = lax.broadcasted_iota(jnp.int32, shape, column_dim)
    patch = lax.broadcasted_iota(jnp.int32, shape, 1 - column_dim)
    hit = column == 2 * patch + (parity + offset)
    return jnp.where(hit, 1.0, 0.0).astype(jnp.bfloat16)


def dot(a, b):
    return jnp.dot(a, b, preferred_element_type=jnp.float32)


def branch_kernel(
    offset_ref, own, auxs, mod, w_patch, full, w_out_hbm, w_final, out, pat, hid, rstd, att, w_out, sem
):
    load = pltpu.make_async_copy(w_out_hbm, w_out, sem)
    load.start()
    offset = offset_ref[0]
    area, columns = own.shape
    channels = w_patch.shape[0] // 4
    band = 2 * channels
    wide = jnp.concatenate([own[...], auxs[0, :area], auxs[1, :area]], axis=1).astype(jnp.bfloat16)
    spread = [dot(wide, column_map((3 * columns, columns), 0, b, offset)) for b in range(2)]
    for p in range(area // band):
        block = jnp.concatenate(
            [
                spread[b][p * band + a * channels : p * band + (a + 1) * channels]
                for a in range(2)
                for b in range(2)
            ],
            axis=0,
        )
        pat[p * columns : (p + 1) * columns] = block.T.astype(jnp.bfloat16)
    hid[...] = dot(pat[...], w_patch[...])
    hidden = hid[...]
    centered = hidden - jnp.mean(hidden, axis=1, keepdims=True)
    rstd[...] = jnp.broadcast_to(
        lax.rsqrt(jnp.mean(centered * centered, axis=1, keepdims=True) + epsilon), rstd.shape
    )
    features = w_patch.shape[0]
    size = full.shape[2]
    each = w_out.shape[0] // size
    row_head = lax.broadcasted_iota(jnp.int32, (size, size), 0) // HEAD
    col_head = lax.broadcasted_iota(jnp.int32, (size, size), 1) // HEAD
    same_head = jnp.where(row_head == col_head, 1.0 / HEAD, 0.0).astype(jnp.bfloat16)
    scale = math.log2(math.e) / math.sqrt(HEAD)
    ones = jnp.ones((pat.shape[0], HEAD), jnp.bfloat16)

    def project(i):
        block = full[i]
        return dot(pat[...], block[:features]) * rstd[:, :1] + block[features : features + 1].astype(
            jnp.float32
        )

    def head_norm(values):
        square = dot((values * values).astype(jnp.bfloat16), same_head)
        return values * lax.rsqrt(square + epsilon)

    @pl.loop(0, each)
    def _(j):
        queries = (head_norm(project(j)) * scale).astype(jnp.bfloat16)
        keys = head_norm(project(each + j)).astype(jnp.bfloat16)
        values = project(2 * each + j).astype(jnp.bfloat16)
        mixed = []
        for h in range(size // HEAD):
            cut = slice(h * HEAD, (h + 1) * HEAD)
            scores = lax.dot_general(
                queries[:, cut], keys[:, cut], (((1,), (1,)), ((), ())),
                preferred_element_type=jnp.float32,
            )
            weights = jnp.exp2(scores).astype(jnp.bfloat16)
            sums = dot(weights, jnp.concatenate([values[:, cut], ones], axis=1))
            mixed.append(sums[:, :HEAD] / sums[:, HEAD:])
        att[:, pl.ds(pl.multiple_of(j * size, LANES), size)] = jnp.concatenate(mixed, axis=1).astype(
            jnp.bfloat16
        )

    load.wait()
    step = 2 * columns
    for start in range(0, pat.shape[0], step):
        rows = slice(start, start + step)
        residual = hid[rows] + mod[2:3] * dot(att[rows], w_out[...])
        centered = residual - jnp.mean(residual, axis=1, keepdims=True)
        spread_of = jnp.mean(centered * centered, axis=1, keepdims=True)
        final_in = (centered * lax.rsqrt(spread_of + epsilon)).astype(jnp.bfloat16)
        tokens = dot(final_in, w_final[...])
        for i in range(step // columns):
            p = start // columns + i
            turned = tokens[i * columns : (i + 1) * columns].T.astype(jnp.bfloat16)
            laid = [dot(turned, column_map((columns, 3 * columns), 1, b, offset)) for b in range(2)]
            for a in range(2):
                low = a * band
                out[p * band + a * channels : p * band + (a + 1) * channels] = (
                    laid[0][low : low + channels] + laid[1][low + channels : low + band]
                ).astype(jnp.bfloat16)


def branch_velocity(offset, own, auxs, mod, w_patch, full, w_out, w_final):
    area, columns = own.shape
    tokens = area * 2 * columns // w_patch.shape[0]
    width = w_patch.shape[1]
    vmem = pl.BlockSpec(memory_space=pltpu.VMEM)
    return pl.pallas_call(
        branch_kernel,
        name="branch_velocity",
        out_shape=jax.ShapeDtypeStruct((area, 3 * columns), jnp.bfloat16),
        in_specs=[pl.BlockSpec(memory_space=pltpu.SMEM)]
        + [vmem] * 5
        + [pl.BlockSpec(memory_space=pl.ANY), vmem],
        out_specs=vmem,
        scratch_shapes=[
            pltpu.VMEM((tokens, w_patch.shape[0]), jnp.bfloat16),
            pltpu.VMEM((tokens, width), jnp.float32),
            pltpu.VMEM((tokens, LANES), jnp.float32),
            pltpu.VMEM((tokens, w_out.shape[0]), jnp.bfloat16),
            pltpu.VMEM(w_out.shape, w_out.dtype),
            pltpu.SemaphoreType.DMA,
        ],
        compiler_params=pltpu.CompilerParams(vmem_limit_bytes=56 << 20),
    )(offset, own, auxs, mod, w_patch, full, w_out, w_final)


def blend_kernel(
    n, sigma, v, own, counts, auxs, clean, border, other, outgoing, incoming, send_v, recv_v, send, recv
):
    g = lax.axis_index("groups")
    w = lax.axis_index("width")
    e = lax.axis_index("guide")
    area, columns = own.shape
    barrier = pltpu.get_barrier_semaphore()

    def place(shift):
        return at(g, lax.rem(w + shift + n, n))

    pl.semaphore_signal(barrier, inc=1, device_id={"guide": 1 - e}, device_id_type=MESH)
    for shift in (-2, -1, 1, 2):
        pl.semaphore_signal(barrier, inc=1, device_id=place(shift), device_id_type=MESH)
    pl.semaphore_wait(barrier, 5)
    swap = pltpu.make_async_remote_copy(
        src_ref=v, dst_ref=other, send_sem=send_v, recv_sem=recv_v,
        device_id={"guide": 1 - e}, device_id_type=MESH,
    )
    swap.start()
    swap.wait()
    mine = v[...].astype(jnp.float32)
    theirs = other[...].astype(jnp.float32)
    first = e == 0
    with_text = jnp.where(first, mine, theirs)
    plain = jnp.where(first, theirs, mine)
    guided = plain + guidance * (with_text - plain)
    here, ahead, further = (guided[:, i * columns : (i + 1) * columns] for i in range(3))
    lane = lax.broadcasted_iota(jnp.int32, (area, columns), 1)
    at_end = lane == columns - 1
    outgoing[0] = ahead.astype(jnp.bfloat16)
    outgoing[1] = jnp.where(at_end, here, further).astype(jnp.bfloat16)
    outgoing[2] = jnp.where(at_end, ahead, further).astype(jnp.bfloat16)
    outgoing[3] = here.astype(jnp.bfloat16)
    moves = [
        pltpu.make_async_remote_copy(
            src_ref=outgoing.at[i], dst_ref=incoming.at[i],
            send_sem=send.at[i], recv_sem=recv.at[i],
            device_id=place(shift), device_id_type=MESH,
        )
        for i, shift in enumerate((1, 1, 2, -1))
    ]
    for move in moves:
        move.start()
    for move in moves:
        move.wait()
    got = [incoming[i].astype(jnp.float32) for i in range(4)]
    total = here + got[0] + jnp.where(at_end, 0.0, got[2])
    clean[...] = own[...] - sigma[0] * (total / counts[:1])
    around = jnp.where(at_end, got[1] + got[2], got[3] + ahead + got[1])
    row_end = lax.broadcasted_iota(jnp.int32, (1, columns), 1) == columns - 1
    covered = jnp.where(row_end, auxs[2, area : area + 1], auxs[0, area : area + 1])
    latent = jnp.where(at_end, auxs[2, :area], auxs[0, :area])
    left = jnp.where(w > 0, 1.0, 0.0)
    right = jnp.where(w < n - 1, 1.0, 0.0)
    inside = jnp.where(at_end, left, right)
    border[...] = inside * (latent - sigma[0] * (around / covered))


def blend(n, sigma, v, own, counts, auxs):
    vmem = pl.BlockSpec(memory_space=pltpu.VMEM)
    dma = pltpu.SemaphoreType.DMA
    return pl.pallas_call(
        functools.partial(blend_kernel, n),
        name="blend",
        out_shape=(jax.ShapeDtypeStruct(own.shape, own.dtype),) * 2,
        in_specs=[pl.BlockSpec(memory_space=pltpu.SMEM)] + [vmem] * 4,
        out_specs=(vmem, vmem),
        scratch_shapes=[
            pltpu.VMEM(v.shape, v.dtype),
            pltpu.VMEM((4, *own.shape), jnp.bfloat16),
            pltpu.VMEM((4, *own.shape), jnp.bfloat16),
            dma, dma, dma((4,)), dma((4,)),
        ],
        compiler_params=pltpu.CompilerParams(
            collective_id=1, has_side_effects=True, vmem_limit_bytes=16 << 20
        ),
    )(sigma, v, own, counts, auxs)


def convolve(padded, w_dec):
    channels = padded.shape[0]
    height = padded.shape[1] - 2
    breadth = padded.shape[2] - 2
    shifted = [
        padded[:, row_at : row_at + height, col_at : col_at + breadth]
        for row_at in range(3)
        for col_at in range(3)
    ]
    stacked = jnp.stack(shifted).reshape(9 * channels, height * breadth)
    summed = lax.dot_general(
        stacked, w_dec, (((0,), (0,)), ((), ())), preferred_element_type=jnp.float32
    )
    return jax.nn.silu(summed).astype(jnp.bfloat16).reshape(height, breadth, w_dec.shape[1])


def shards(latent, starts, counts, step_index, cond_mod, w_patch, w_qkv, w_out, w_final, w_dec):
    groups, n = lax.axis_size("groups"), lax.axis_size("width")
    guide_at = lax.axis_index("guide")
    place = lax.axis_index("width")
    channels, height, columns = latent.shape
    half_rows = height // 2
    fraction = (step_index.astype(jnp.float32) + 1.0) / STEPS
    sigma = 3.0 * fraction / (1.0 + 2.0 * fraction)
    modulation = cond_mod[0]
    area = height * channels
    own = latent.transpose(1, 0, 2).reshape(area, columns)
    cover = jnp.broadcast_to(counts.astype(jnp.float32)[None], (8, columns))
    aux = jnp.concatenate([own, cover], axis=0)
    lhs = fold_rows(modulation, w_patch, w_qkv.shape[0], place)
    full, auxs = gather_folded(groups, n, lhs, w_qkv, aux)
    offset = starts - place * columns
    velocity = branch_velocity(offset, own, auxs, modulation, w_patch, full, w_out, w_final)
    clean, border = blend(n, sigma, velocity, own, cover, auxs)
    rows = clean.reshape(height, channels, columns)
    sides = border.reshape(height, channels, columns)
    denoised = lax.dynamic_slice_in_dim(rows, guide_at * half_rows, half_rows, 0).transpose(1, 0, 2)
    padded = jnp.concatenate([sides[:, :, -1:], rows, sides[:, :, :1]], axis=2).astype(jnp.bfloat16)
    padded = jnp.pad(padded, ((1, 1), (0, 0), (0, 0)))
    padded = lax.dynamic_slice_in_dim(padded, guide_at * half_rows, half_rows + 2, 0)
    features = convolve(padded.transpose(1, 0, 2), w_dec)
    return (denoised, features)


def solution(mesh):
    return jax.shard_map(
        shards,
        mesh=mesh,
        in_specs=(
            P(None, None, ("groups", "width")),
            P(("groups", "width")),
            P(("groups", "width")),
            P("groups"),
            P("guide", None, None),
            P(),
            P("width", None),
            P(),
            P(),
            P(),
        ),
        out_specs=(P(None, "guide", ("groups", "width")), P("guide", ("groups", "width"), None)),
        check_vma=False,
    )
```

```python
import functools
import math

import jax
import jax.numpy as jnp
from jax import lax
from jax.experimental import pallas as pl
from jax.experimental.pallas import tpu as pltpu
from jax.sharding import PartitionSpec as P

HEAD = 64
STEPS = 28
LANES = 128
MESH = pl.DeviceIdType.MESH

guidance = 4.0
epsilon = 1e-06


def at(groups, width):
    return {"groups": groups, "width": width}


def column_map(shape, column_dim, parity, offset):
    column = lax.broadcasted_iota(jnp.int32, shape, column_dim)
    patch = lax.broadcasted_iota(jnp.int32, shape, 1 - column_dim)
    hit = column == 2 * patch + (parity + offset)
    return jnp.where(hit, 1.0, 0.0).astype(jnp.bfloat16)


def dot(a, b):
    return jnp.dot(a, b, preferred_element_type=jnp.float32)


def row_map(shape, natural_dim, channels, height):
    natural = lax.broadcasted_iota(jnp.int32, shape, natural_dim)
    moved = lax.broadcasted_iota(jnp.int32, shape, 1 - natural_dim)
    hit = natural == lax.rem(moved, channels) * height + moved // channels
    return jnp.where(hit, 1.0, 0.0).astype(jnp.bfloat16)


def fold_rows(modulation, w_patch, depth, w):
    patch = w_patch[...].astype(jnp.float32)
    patch = patch - jnp.mean(patch, axis=1, keepdims=True)
    shift = jnp.broadcast_to(modulation[0:1], (16, patch.shape[1]))
    rows = jnp.concatenate([patch * (1.0 + modulation[1:2]), shift], axis=0)
    total = rows.shape[1]
    rows = pltpu.roll(rows, lax.rem(total - w * depth, total), 1)[:, :depth]
    high = rows.astype(jnp.bfloat16)
    return high, (rows - high.astype(jnp.float32)).astype(jnp.bfloat16)


def step_kernel(
    groups, n,
    offset_ref, sigma, latent, counts, mod, w_patch, w_final, w_qkv_hbm, w_out_hbm,
    clean, border,
    w_qkv, w_out, high, low, soft, edges, softs, edge_pair, parts, arrived, full, shifts,
    pat, rstd, att, turned_v, v, other, outgoing, incoming,
    load_sem, send_a, recv_a, send_b, recv_b, send_x, recv_x, send_v, recv_v, send, recv,
):
    g = lax.axis_index("groups")
    w = lax.axis_index("width")
    e = lax.axis_index("guide")
    owners = groups * n
    me = g * n + w
    features, size = full.shape[1:]
    area, columns = latent.shape
    channels = features // 4
    height = area // channels
    band = 2 * channels
    pieces = w_qkv.shape[1] // size
    barrier = pltpu.get_barrier_semaphore()

    @pl.loop(1, owners)
    def _(step):
        to = lax.rem(me + step, owners)
        pl.semaphore_signal(
            barrier, inc=1, device_id=at(to // n, lax.rem(to, n)), device_id_type=MESH
        )

    pl.semaphore_signal(barrier, inc=1, device_id={"guide": 1 - e}, device_id_type=MESH)
    load_qkv = pltpu.make_async_copy(w_qkv_hbm, w_qkv, load_sem.at[0])
    load_out = pltpu.make_async_copy(w_out_hbm, w_out, load_sem.at[1])
    load_qkv.start()
    load_out.start()

    own = latent[...]
    soft[...] = own.astype(jnp.bfloat16)
    turned = own.T
    cover = counts[...].astype(jnp.float32)
    edges[...] = jnp.concatenate(
        [turned[:1], turned[columns - 1 :], cover, jnp.zeros((5, columns), jnp.float32)], axis=0
    )
    high_rows, low_rows = fold_rows(mod, w_patch, w_qkv.shape[0], w)
    high[...] = high_rows
    low[...] = low_rows
    load_qkv.wait()

    @pl.loop(0, n)
    def _(step):
        chunk = jnp.minimum(g * n + lax.rem(w + step, n), pieces - 1)
        cut = w_qkv[:, pl.ds(pl.multiple_of(chunk * size, LANES), size)]
        parts[step] = (dot(high[:features], cut) + dot(low[:features], cut)).astype(jnp.bfloat16)

    @pl.when(g == pieces // n)
    def _():
        line = dot(high[features:], w_qkv[...]) + dot(low[features:], w_qkv[...])
        lines = jnp.concatenate([line[:1, i * size : (i + 1) * size] for i in range(pieces)], axis=0)
        lines = jnp.concatenate(
            [lines, jnp.zeros((features - pieces, size), jnp.float32)], axis=0
        )
        parts[lax.rem(pieces % n - w + n, n)] = lines.astype(jnp.bfloat16)

    pl.semaphore_wait(barrier, owners)

    def remote(source, target, sent, received, shift):
        return pltpu.make_async_remote_copy(
            src_ref=source, dst_ref=target, send_sem=sent, recv_sem=received,
            device_id=at(g, lax.rem(w + shift + n, n)), device_id_type=MESH,
        )

    def scatter(step):
        return remote(parts.at[step], arrived.at[step], send_a.at[step], recv_a.at[step], step)

    @pl.loop(1, n)
    def _(step):
        scatter(step).start()

    moves = [
        remote(soft, softs.at[0], send_x.at[0], recv_x.at[0], -1),
        remote(soft, softs.at[1], send_x.at[1], recv_x.at[1], -2),
        remote(edges, edge_pair.at[0], send_x.at[2], recv_x.at[2], -1),
        remote(edges, edge_pair.at[1], send_x.at[3], recv_x.at[3], 1),
    ]
    for move in moves:
        move.start()

    @pl.loop(1, n)
    def _(step):
        scatter(step).wait_recv()

    def add(step, total):
        return total + arrived[step].astype(jnp.float32)

    full[me] = lax.fori_loop(1, n, add, parts[0].astype(jnp.float32)).astype(jnp.bfloat16)

    def shared(step, peer, source):
        return pltpu.make_async_remote_copy(
            src_ref=full.at[source], dst_ref=full.at[source],
            send_sem=send_b.at[step], recv_sem=recv_b.at[step],
            device_id=at(peer // n, lax.rem(peer, n)), device_id_type=MESH,
        )

    @pl.loop(1, owners)
    def _(step):
        shared(step, lax.rem(me + step, owners), me).start()

    for move in moves:
        move.wait()
    offset = offset_ref[0]
    wide = jnp.concatenate([soft[...], softs[0], softs[1]], axis=1)
    wide = dot(row_map((area, area), 1, channels, height), wide).astype(jnp.bfloat16)
    spread = [dot(wide, column_map((3 * columns, columns), 0, b, offset)) for b in range(2)]
    for p in range(area // band):
        block = jnp.concatenate(
            [
                spread[b][p * band + a * channels : p * band + (a + 1) * channels]
                for a in range(2)
                for b in range(2)
            ],
            axis=0,
        )
        pat[p * columns : (p + 1) * columns] = block.T.astype(jnp.bfloat16)
    tokens = pat.shape[0]
    step_rows = 2 * columns
    for start in range(0, tokens, step_rows):
        rows = slice(start, start + step_rows)
        hidden = dot(pat[rows], w_patch[...])
        centered = hidden - jnp.mean(hidden, axis=1, keepdims=True)
        rstd[rows] = jnp.broadcast_to(
            lax.rsqrt(jnp.mean(centered * centered, axis=1, keepdims=True) + epsilon),
            (step_rows, rstd.shape[1]),
        )
    each = w_out.shape[0] // size
    row_head = lax.broadcasted_iota(jnp.int32, (size, size), 0) // HEAD
    col_head = lax.broadcasted_iota(jnp.int32, (size, size), 1) // HEAD
    same_head = jnp.where(row_head == col_head, 1.0 / HEAD, 0.0).astype(jnp.bfloat16)
    scale = math.log2(math.e) / math.sqrt(HEAD)
    ones = jnp.ones((tokens, HEAD), jnp.bfloat16)

    @pl.loop(1, owners)
    def _(step):
        source = lax.rem(me - step + owners, owners)
        shared(step, source, source).wait_recv()

    shifts[...] = full[pieces].astype(jnp.float32)

    def project(i):
        return dot(pat[...], full[i]) * rstd[:, :1] + shifts[pl.ds(i, 1)]

    def head_norm(values):
        square = dot((values * values).astype(jnp.bfloat16), same_head)
        return values * lax.rsqrt(square + epsilon)

    @pl.loop(0, each)
    def _(j):
        queries = (head_norm(project(j)) * scale).astype(jnp.bfloat16)
        keys = head_norm(project(each + j)).astype(jnp.bfloat16)
        values = project(2 * each + j).astype(jnp.bfloat16)
        mixed = []
        for h in range(size // HEAD):
            cut = slice(h * HEAD, (h + 1) * HEAD)
            scores = lax.dot_general(
                queries[:, cut], keys[:, cut], (((1,), (1,)), ((), ())),
                preferred_element_type=jnp.float32,
            )
            weights = jnp.exp2(scores).astype(jnp.bfloat16)
            sums = dot(weights, jnp.concatenate([values[:, cut], ones], axis=1))
            mixed.append(sums[:, :HEAD] / sums[:, HEAD:])
        att[:, pl.ds(pl.multiple_of(j * size, LANES), size)] = jnp.concatenate(mixed, axis=1).astype(
            jnp.bfloat16
        )

    load_out.wait()
    for start in range(0, tokens, step_rows):
        rows = slice(start, start + step_rows)
        residual = dot(pat[rows], w_patch[...]) + mod[2:3] * dot(att[rows], w_out[...])
        centered = residual - jnp.mean(residual, axis=1, keepdims=True)
        spread_of = jnp.mean(centered * centered, axis=1, keepdims=True)
        final_in = (centered * lax.rsqrt(spread_of + epsilon)).astype(jnp.bfloat16)
        found = lax.dot_general(
            final_in, w_final[...], (((1,), (1,)), ((), ())), preferred_element_type=jnp.float32
        )
        for i in range(step_rows // columns):
            p = start // columns + i
            turned = found[i * columns : (i + 1) * columns].T.astype(jnp.bfloat16)
            laid = [dot(turned, column_map((columns, 3 * columns), 1, b, offset)) for b in range(2)]
            for a in range(2):
                at_row = a * band
                turned_v[p * band + a * channels : p * band + (a + 1) * channels] = (
                    laid[0][at_row : at_row + channels] + laid[1][at_row + channels : at_row + band]
                ).astype(jnp.bfloat16)
    v[...] = dot(row_map((area, area), 0, channels, height), turned_v[...]).astype(jnp.bfloat16)

    swap = pltpu.make_async_remote_copy(
        src_ref=v, dst_ref=other, send_sem=send_v, recv_sem=recv_v,
        device_id={"guide": 1 - e}, device_id_type=MESH,
    )
    swap.start()
    swap.wait()
    mine = v[...].astype(jnp.float32)
    theirs = other[...].astype(jnp.float32)
    first = e == 0
    with_text = jnp.where(first, mine, theirs)
    plain = jnp.where(first, theirs, mine)
    guided = plain + guidance * (with_text - plain)
    here, ahead, further = (guided[:, i * columns : (i + 1) * columns] for i in range(3))
    at_end = lax.broadcasted_iota(jnp.int32, (area, columns), 1) == columns - 1
    outgoing[0] = ahead.astype(jnp.bfloat16)
    outgoing[1] = jnp.where(at_end, here, further).astype(jnp.bfloat16)
    outgoing[2] = jnp.where(at_end, ahead, further).astype(jnp.bfloat16)
    outgoing[3] = here.astype(jnp.bfloat16)
    moves = [
        remote(outgoing.at[i], incoming.at[i], send.at[i], recv.at[i], shift)
        for i, shift in enumerate((1, 1, 2, -1))
    ]
    for move in moves:
        move.start()

    @pl.loop(1, n)
    def _(step):
        scatter(step).wait_send()

    @pl.loop(1, owners)
    def _(step):
        shared(step, lax.rem(me + step, owners), me).wait_send()

    for move in moves:
        move.wait()
    got = [incoming[i].astype(jnp.float32) for i in range(4)]
    total = here + got[0] + jnp.where(at_end, 0.0, got[2])
    clean[...] = own - sigma[0] * (total / cover)
    around = jnp.where(at_end, got[1] + got[2], got[3] + ahead + got[1])
    row_end = lax.broadcasted_iota(jnp.int32, (1, columns), 1) == columns - 1
    right_edges, left_edges = edge_pair[0], edge_pair[1]
    covered = jnp.where(row_end, left_edges[2:3], right_edges[2:3])
    beside = jnp.where(at_end, left_edges.T[:, 1:2], right_edges.T[:, 0:1])
    left = jnp.where(w > 0, 1.0, 0.0)
    right = jnp.where(w < n - 1, 1.0, 0.0)
    border[...] = jnp.where(at_end, left, right) * (beside - sigma[0] * (around / covered))


def run_step(groups, n, offset, sigma, own, counts, mod, w_patch, w_final, w_qkv, w_out):
    total = w_qkv.shape[1]
    owners = groups * n
    size = LANES * -(-total // (LANES * owners))
    while (total // 3) % size or total // size >= owners:
        size += LANES
    area, columns = own.shape
    features = w_patch.shape[0]
    tokens = area * 2 * columns // features
    dma = pltpu.SemaphoreType.DMA
    vmem = pl.BlockSpec(memory_space=pltpu.VMEM)
    smem = pl.BlockSpec(memory_space=pltpu.SMEM)
    hbm = pl.BlockSpec(memory_space=pl.ANY)
    half, single = jnp.bfloat16, jnp.float32
    return pl.pallas_call(
        functools.partial(step_kernel, groups, n),
        name="guided_step",
        out_shape=(jax.ShapeDtypeStruct(own.shape, own.dtype),) * 2,
        in_specs=[smem] * 2 + [vmem] * 5 + [hbm] * 2,
        out_specs=(vmem, vmem),
        scratch_shapes=[
            pltpu.VMEM(w_qkv.shape, half),
            pltpu.VMEM(w_out.shape, half),
            pltpu.VMEM((features + 16, w_qkv.shape[0]), half),
            pltpu.VMEM((features + 16, w_qkv.shape[0]), half),
            pltpu.VMEM(own.shape, half),
            pltpu.VMEM((8, columns), single),
            pltpu.VMEM((2, *own.shape), half),
            pltpu.VMEM((2, 8, columns), single),
            pltpu.VMEM((n, features, size), half),
            pltpu.VMEM((n, features, size), half),
            pltpu.VMEM((owners, features, size), half),
            pltpu.VMEM((features, size), single),
            pltpu.VMEM((tokens, features), half),
            pltpu.VMEM((tokens, LANES), single),
            pltpu.VMEM((tokens, w_out.shape[0]), half),
            pltpu.VMEM((area, 3 * columns), half),
            pltpu.VMEM((area, 3 * columns), half),
            pltpu.VMEM((area, 3 * columns), half),
            pltpu.VMEM((4, *own.shape), half),
            pltpu.VMEM((4, *own.shape), half),
            dma((2,)), dma((n,)), dma((n,)), dma((owners,)), dma((owners,)), dma((4,)), dma((4,)),
            dma, dma, dma((4,)), dma((4,)),
        ],
        compiler_params=pltpu.CompilerParams(
            collective_id=0, has_side_effects=True, vmem_limit_bytes=56 << 20
        ),
    )(offset, sigma, own, counts, mod, w_patch, w_final, w_qkv, w_out)


def convolve(padded, w_dec):
    channels = padded.shape[0]
    height = padded.shape[1] - 2
    breadth = padded.shape[2] - 2
    shifted = [
        padded[:, row_at : row_at + height, col_at : col_at + breadth]
        for row_at in range(3)
        for col_at in range(3)
    ]
    stacked = jnp.stack(shifted).reshape(9 * channels, height * breadth)
    summed = lax.dot_general(
        stacked, w_dec, (((0,), (0,)), ((), ())), preferred_element_type=jnp.float32
    )
    return jax.nn.silu(summed).astype(jnp.bfloat16).reshape(height, breadth, w_dec.shape[1])


def shards(latent, starts, counts, step_index, cond_mod, w_patch, w_qkv, w_out, w_final, w_dec):
    groups, n = lax.axis_size("groups"), lax.axis_size("width")
    guide_at = lax.axis_index("guide")
    place = lax.axis_index("width")
    channels, height, columns = latent.shape
    half_rows = height // 2
    fraction = (step_index.astype(jnp.float32) + 1.0) / STEPS
    sigma = 3.0 * fraction / (1.0 + 2.0 * fraction)
    own = latent.reshape(channels * height, columns)
    offset = starts - place * columns
    clean, border = run_step(
        groups, n, offset, sigma, own, counts[None], cond_mod[0], w_patch, w_final.T, w_qkv, w_out
    )
    rows = clean.reshape(latent.shape)
    sides = border.reshape(latent.shape)
    denoised = lax.dynamic_slice_in_dim(rows, guide_at * half_rows, half_rows, 1)
    padded = jnp.concatenate([sides[:, :, -1:], rows, sides[:, :, :1]], axis=2).astype(jnp.bfloat16)
    padded = jnp.pad(padded, ((0, 0), (1, 1), (0, 0)))
    padded = lax.dynamic_slice_in_dim(padded, guide_at * half_rows, half_rows + 2, 1)
    features = convolve(padded, w_dec)
    return (denoised, features)


def solution(mesh):
    return jax.shard_map(
        shards,
        mesh=mesh,
        in_specs=(
            P(None, None, ("groups", "width")),
            P(("groups", "width")),
            P(("groups", "width")),
            P("groups"),
            P("guide", None, None),
            P(),
            P("width", None),
            P(),
            P(),
            P(),
        ),
        out_specs=(P(None, "guide", ("groups", "width")), P("guide", ("groups", "width"), None)),
        check_vma=False,
    )
```

```python
import functools
import math

import jax
import jax.numpy as jnp
from jax import lax
from jax.experimental import pallas as pl
from jax.experimental.pallas import tpu as pltpu
from jax.sharding import PartitionSpec as P

HEAD = 64
STEPS = 28
LANES = 128
MESH = pl.DeviceIdType.MESH

guidance = 4.0
epsilon = 1e-06


def at(groups, width):
    return {"groups": groups, "width": width}


def column_map(shape, column_dim, parity, offset):
    column = lax.broadcasted_iota(jnp.int32, shape, column_dim)
    patch = lax.broadcasted_iota(jnp.int32, shape, 1 - column_dim)
    hit = column == 2 * patch + (parity + offset)
    return jnp.where(hit, 1.0, 0.0).astype(jnp.bfloat16)


def dot(a, b):
    return jnp.dot(a, b, preferred_element_type=jnp.float32)


def row_map(shape, natural_dim, channels, height):
    natural = lax.broadcasted_iota(jnp.int32, shape, natural_dim)
    moved = lax.broadcasted_iota(jnp.int32, shape, 1 - natural_dim)
    hit = natural == lax.rem(moved, channels) * height + moved // channels
    return jnp.where(hit, 1.0, 0.0).astype(jnp.bfloat16)


def fold_rows(modulation, w_patch, depth, w):
    patch = w_patch[...].astype(jnp.float32)
    patch = patch - jnp.mean(patch, axis=1, keepdims=True)
    shift = jnp.broadcast_to(modulation[0], (16, patch.shape[1]))
    rows = jnp.concatenate([patch * (1.0 + modulation[1]), shift], axis=0)
    total = rows.shape[1]
    rows = pltpu.roll(rows, lax.rem(total - w * depth, total), 1)[:, :depth]
    high = rows.astype(jnp.bfloat16)
    return high, (rows - high.astype(jnp.float32)).astype(jnp.bfloat16)


def step_kernel(
    groups, n,
    starts, step_index, latent, counts, mod, w_patch, w_final, w_qkv_hbm, w_out_hbm,
    clean, border,
    w_qkv, w_out, high, low, soft, edges, softs, edge_pair, parts, arrived, full, shifts,
    pat, rstd, att, turned_v, v, other, outgoing, incoming,
    load_sem, send_a, recv_a, send_c, send_b, recv_b, send_x, recv_x, send_v, recv_v, send, recv,
):
    g = lax.axis_index("groups")
    w = lax.axis_index("width")
    e = lax.axis_index("guide")
    owners = groups * n
    me = g * n + w
    features, size = full.shape[1:]
    area, columns = latent.shape
    channels = features // 4
    height = area // channels
    band = 2 * channels
    pieces = w_qkv.shape[1] // size
    barrier = pltpu.get_barrier_semaphore()

    @pl.loop(1, owners)
    def _(step):
        to = lax.rem(me + step, owners)
        pl.semaphore_signal(
            barrier, inc=1, device_id=at(to // n, lax.rem(to, n)), device_id_type=MESH
        )

    pl.semaphore_signal(barrier, inc=1, device_id={"guide": 1 - e}, device_id_type=MESH)
    load_qkv = pltpu.make_async_copy(w_qkv_hbm, w_qkv, load_sem.at[0])
    load_out = pltpu.make_async_copy(w_out_hbm, w_out, load_sem.at[1])
    load_qkv.start()
    load_out.start()

    own = latent[...]
    soft[...] = own.astype(jnp.bfloat16)
    turned = own.T
    index = jnp.full((1, columns), step_index[0], jnp.int32).astype(jnp.float32)
    fraction = (index + 1.0) / STEPS
    sigma = 3.0 * fraction / (1.0 + 2.0 * fraction)
    cover = counts[...].astype(jnp.float32)
    edges[...] = jnp.concatenate(
        [turned[:1], turned[columns - 1 :], cover, jnp.zeros((5, columns), jnp.float32)], axis=0
    )
    high_rows, low_rows = fold_rows(mod, w_patch, w_qkv.shape[0], w)
    high[...] = high_rows
    low[...] = low_rows
    load_qkv.wait()

    @pl.loop(0, n)
    def _(step):
        chunk = jnp.minimum(g * n + lax.rem(w + step, n), pieces - 1)
        cut = w_qkv[:, pl.ds(pl.multiple_of(chunk * size, LANES), size)]
        parts[step] = (dot(high[:features], cut) + dot(low[:features], cut)).astype(jnp.bfloat16)

    @pl.when(g == pieces // n)
    def _():
        line = dot(high[features:], w_qkv[...]) + dot(low[features:], w_qkv[...])
        lines = jnp.concatenate([line[:1, i * size : (i + 1) * size] for i in range(pieces)], axis=0)
        lines = jnp.concatenate(
            [lines, jnp.zeros((features - pieces, size), jnp.float32)], axis=0
        )
        parts[lax.rem(pieces % n - w + n, n)] = lines.astype(jnp.bfloat16)

    pl.semaphore_wait(barrier, owners)

    def remote(source, target, sent, received, shift):
        return pltpu.make_async_remote_copy(
            src_ref=source, dst_ref=target, send_sem=sent, recv_sem=received,
            device_id=at(g, lax.rem(w + shift + n, n)), device_id_type=MESH,
        )

    def scatter(step):
        return remote(parts.at[step], arrived.at[step], send_a.at[step], recv_a.at[step], step)

    @pl.loop(1, n)
    def _(step):
        scatter(step).start()

    moves = [
        remote(soft, softs.at[0], send_x.at[0], recv_x.at[0], -1),
        remote(soft, softs.at[1], send_x.at[1], recv_x.at[1], -2),
        remote(edges, edge_pair.at[0], send_x.at[2], recv_x.at[2], -1),
        remote(edges, edge_pair.at[1], send_x.at[3], recv_x.at[3], 1),
    ]
    for move in moves:
        move.start()

    @pl.loop(1, n)
    def _(step):
        scatter(step).wait_recv()

    def add(step, total):
        return total + arrived[step].astype(jnp.float32)

    full[me] = lax.fori_loop(1, n, add, parts[0].astype(jnp.float32)).astype(jnp.bfloat16)

    deep = n // 2
    sides = 2 * groups
    side = g * 2 + lax.rem(w, 2)
    level = w // 2

    def owner_of(which_side, which_level):
        return (which_side // 2) * n + which_level * 2 + lax.rem(which_side, 2)

    def passed(source, peer, sent):
        return pltpu.make_async_remote_copy(
            src_ref=full.at[source], dst_ref=full.at[source], send_sem=sent, recv_sem=recv_b.at[source],
            device_id=at(peer // n, lax.rem(peer, n)), device_id_type=MESH,
        )

    def along(step):
        return passed(me, owner_of(side, lax.rem(level + step, deep)), send_c.at[step])

    def aside(step, turn):
        source = owner_of(side, lax.rem(level + step, deep))
        peer = owner_of(lax.rem(side + turn, sides), level)
        return passed(source, peer, send_b.at[step, turn])

    @pl.loop(1, deep)
    def _(step):
        along(step).start()

    @pl.loop(1, sides)
    def _(turn):
        aside(0, turn).start()

    for move in moves:
        move.wait()
    offset = starts[0] - w * columns
    wide = jnp.concatenate([soft[...], softs[0], softs[1]], axis=1)
    wide = dot(row_map((area, area), 1, channels, height), wide).astype(jnp.bfloat16)
    spread = [dot(wide, column_map((3 * columns, columns), 0, b, offset)) for b in range(2)]
    for p in range(area // band):
        block = jnp.concatenate(
            [
                spread[b][p * band + a * channels : p * band + (a + 1) * channels]
                for a in range(2)
                for b in range(2)
            ],
            axis=0,
        )
        pat[p * columns : (p + 1) * columns] = block.T.astype(jnp.bfloat16)

    @pl.loop(1, deep)
    def _(step):
        source = owner_of(side, lax.rem(level + step, deep))
        passed(source, source, send_c.at[step]).wait_recv()

        @pl.loop(1, sides)
        def _(turn):
            aside(step, turn).start()

    tokens = pat.shape[0]
    step_rows = 2 * columns
    for start in range(0, tokens, step_rows):
        rows = slice(start, start + step_rows)
        hidden = dot(pat[rows], w_patch[...])
        centered = hidden - jnp.mean(hidden, axis=1, keepdims=True)
        rstd[rows] = jnp.broadcast_to(
            lax.rsqrt(jnp.mean(centered * centered, axis=1, keepdims=True) + epsilon),
            (step_rows, rstd.shape[1]),
        )
    each = w_out.shape[0] // size
    row_head = lax.broadcasted_iota(jnp.int32, (size, size), 0) // HEAD
    col_head = lax.broadcasted_iota(jnp.int32, (size, size), 1) // HEAD
    same_head = jnp.where(row_head == col_head, 1.0 / HEAD, 0.0).astype(jnp.bfloat16)
    scale = math.log2(math.e) / math.sqrt(HEAD)
    ones = jnp.ones((tokens, HEAD), jnp.bfloat16)

    def await_piece(source):
        own_side = (source // n) * 2 + lax.rem(source, 2)

        @pl.when(own_side != side)
        def _():
            passed(source, source, send_c.at[0]).wait_recv()

    @pl.loop(pieces, owners)
    def _(source):
        await_piece(source)

    shifts[...] = full[pieces].astype(jnp.float32)

    def project(i):
        return dot(pat[...], full[i]) * rstd[:, :1] + shifts[pl.ds(i, 1)]

    def head_norm(values):
        square = dot((values * values).astype(jnp.bfloat16), same_head)
        return values * lax.rsqrt(square + epsilon)

    @pl.loop(0, each)
    def _(j):
        for i in range(3):
            await_piece(i * each + j)
        queries = (head_norm(project(j)) * scale).astype(jnp.bfloat16)
        keys = head_norm(project(each + j)).astype(jnp.bfloat16)
        values = project(2 * each + j).astype(jnp.bfloat16)
        mixed = []
        for h in range(size // HEAD):
            cut = slice(h * HEAD, (h + 1) * HEAD)
            scores = lax.dot_general(
                queries[:, cut], keys[:, cut], (((1,), (1,)), ((), ())),
                preferred_element_type=jnp.float32,
            )
            weights = jnp.exp2(scores).astype(jnp.bfloat16)
            sums = dot(weights, jnp.concatenate([values[:, cut], ones], axis=1))
            mixed.append(sums[:, :HEAD] / sums[:, HEAD:])
        att[:, pl.ds(pl.multiple_of(j * size, LANES), size)] = jnp.concatenate(mixed, axis=1).astype(
            jnp.bfloat16
        )

    load_out.wait()
    for start in range(0, tokens, step_rows):
        rows = slice(start, start + step_rows)
        residual = dot(pat[rows], w_patch[...]) + mod[2] * dot(att[rows], w_out[...])
        centered = residual - jnp.mean(residual, axis=1, keepdims=True)
        spread_of = jnp.mean(centered * centered, axis=1, keepdims=True)
        final_in = (centered * lax.rsqrt(spread_of + epsilon)).astype(jnp.bfloat16)
        found = lax.dot_general(
            final_in, w_final[...], (((1,), (1,)), ((), ())), preferred_element_type=jnp.float32
        )
        for i in range(step_rows // columns):
            p = start // columns + i
            turned = found[i * columns : (i + 1) * columns].T.astype(jnp.bfloat16)
            laid = [dot(turned, column_map((columns, 3 * columns), 1, b, offset)) for b in range(2)]
            for a in range(2):
                at_row = a * band
                turned_v[p * band + a * channels : p * band + (a + 1) * channels] = (
                    laid[0][at_row : at_row + channels] + laid[1][at_row + channels : at_row + band]
                ).astype(jnp.bfloat16)
    v[...] = dot(row_map((area, area), 0, channels, height), turned_v[...]).astype(jnp.bfloat16)

    swap = pltpu.make_async_remote_copy(
        src_ref=v, dst_ref=other, send_sem=send_v, recv_sem=recv_v,
        device_id={"guide": 1 - e}, device_id_type=MESH,
    )
    swap.start()
    swap.wait()
    mine = v[...].astype(jnp.float32)
    theirs = other[...].astype(jnp.float32)
    first = e == 0
    with_text = jnp.where(first, mine, theirs)
    plain = jnp.where(first, theirs, mine)
    guided = plain + guidance * (with_text - plain)
    here, ahead, further = (guided[:, i * columns : (i + 1) * columns] for i in range(3))
    at_end = lax.broadcasted_iota(jnp.int32, (area, columns), 1) == columns - 1
    outgoing[0] = ahead.astype(jnp.bfloat16)
    outgoing[1] = jnp.where(at_end, here, further).astype(jnp.bfloat16)
    outgoing[2] = jnp.where(at_end, ahead, further).astype(jnp.bfloat16)
    outgoing[3] = here.astype(jnp.bfloat16)
    moves = [
        remote(outgoing.at[i], incoming.at[i], send.at[i], recv.at[i], shift)
        for i, shift in enumerate((1, 1, 2, -1))
    ]
    for move in moves:
        move.start()

    @pl.loop(1, n)
    def _(step):
        scatter(step).wait_send()

    @pl.loop(1, deep)
    def _(step):
        along(step).wait_send()

    @pl.loop(0, deep)
    def _(step):
        @pl.loop(1, sides)
        def _(turn):
            aside(step, turn).wait_send()

    for move in moves:
        move.wait()
    got = [incoming[i].astype(jnp.float32) for i in range(4)]
    total = here + got[0] + jnp.where(at_end, 0.0, got[2])
    clean[...] = own - sigma * (total / cover)
    around = jnp.where(at_end, got[1] + got[2], got[3] + ahead + got[1])
    row_end = lax.broadcasted_iota(jnp.int32, (1, columns), 1) == columns - 1
    right_edges, left_edges = edge_pair[0], edge_pair[1]
    covered = jnp.where(row_end, left_edges[2:3], right_edges[2:3])
    beside = jnp.where(at_end, left_edges.T[:, 1:2], right_edges.T[:, 0:1])
    left = jnp.where(w > 0, 1.0, 0.0)
    right = jnp.where(w < n - 1, 1.0, 0.0)
    border[...] = jnp.where(at_end, left, right) * (beside - sigma * (around / covered))


def run_step(groups, n, starts, step_index, own, counts, mod, w_patch, w_final, w_qkv, w_out):
    total = w_qkv.shape[1]
    owners = groups * n
    size = LANES * -(-total // (LANES * owners))
    while (total // 3) % size or total // size >= owners:
        size += LANES
    area, columns = own.shape
    features = w_patch.shape[0]
    tokens = area * 2 * columns // features
    dma = pltpu.SemaphoreType.DMA
    vmem = pl.BlockSpec(memory_space=pltpu.VMEM)
    smem = pl.BlockSpec(memory_space=pltpu.SMEM)
    hbm = pl.BlockSpec(memory_space=pl.ANY)
    half, single = jnp.bfloat16, jnp.float32
    return pl.pallas_call(
        functools.partial(step_kernel, groups, n),
        name="guided_step",
        out_shape=(jax.ShapeDtypeStruct(own.shape, own.dtype),) * 2,
        in_specs=[smem] * 2 + [vmem] * 5 + [hbm] * 2,
        out_specs=(vmem, vmem),
        scratch_shapes=[
            pltpu.VMEM(w_qkv.shape, half),
            pltpu.VMEM(w_out.shape, half),
            pltpu.VMEM((features + 16, w_qkv.shape[0]), half),
            pltpu.VMEM((features + 16, w_qkv.shape[0]), half),
            pltpu.VMEM(own.shape, half),
            pltpu.VMEM((8, columns), single),
            pltpu.VMEM((2, *own.shape), half),
            pltpu.VMEM((2, 8, columns), single),
            pltpu.VMEM((n, features, size), half),
            pltpu.VMEM((n, features, size), half),
            pltpu.VMEM((owners, features, size), half),
            pltpu.VMEM((features, size), single),
            pltpu.VMEM((tokens, features), half),
            pltpu.VMEM((tokens, LANES), single),
            pltpu.VMEM((tokens, w_out.shape[0]), half),
            pltpu.VMEM((area, 3 * columns), half),
            pltpu.VMEM((area, 3 * columns), half),
            pltpu.VMEM((area, 3 * columns), half),
            pltpu.VMEM((4, *own.shape), half),
            pltpu.VMEM((4, *own.shape), half),
            dma((2,)), dma((n,)), dma((n,)), dma((n // 2,)), dma((n // 2, 2 * groups)), dma((owners,)), dma((4,)), dma((4,)),
            dma, dma, dma((4,)), dma((4,)),
        ],
        compiler_params=pltpu.CompilerParams(
            collective_id=0, has_side_effects=True, vmem_limit_bytes=56 << 20
        ),
    )(starts, step_index, own, counts, mod, w_patch, w_final, w_qkv, w_out)


def convolve(padded, w_dec):
    channels = padded.shape[0]
    height = padded.shape[1] - 2
    breadth = padded.shape[2] - 2
    shifted = [
        padded[:, row_at : row_at + height, col_at : col_at + breadth]
        for row_at in range(3)
        for col_at in range(3)
    ]
    stacked = jnp.stack(shifted).reshape(9 * channels, height * breadth)
    summed = lax.dot_general(
        stacked, w_dec, (((0,), (0,)), ((), ())), preferred_element_type=jnp.float32
    )
    return jax.nn.silu(summed).astype(jnp.bfloat16).reshape(height, breadth, w_dec.shape[1])


def shards(latent, starts, counts, step_index, cond_mod, w_patch, w_qkv, w_out, w_final, w_dec):
    groups, n = lax.axis_size("groups"), lax.axis_size("width")
    guide_at = lax.axis_index("guide")
    channels, height, columns = latent.shape
    half_rows = height // 2
    own = latent.reshape(channels * height, columns)
    clean, border = run_step(
        groups, n, starts, step_index, own, counts[None], cond_mod.transpose(1, 0, 2), w_patch, w_final.T, w_qkv, w_out
    )
    rows = clean.reshape(latent.shape)
    sides = border.reshape(latent.shape)
    denoised = lax.dynamic_slice_in_dim(rows, guide_at * half_rows, half_rows, 1)
    padded = jnp.concatenate([sides[:, :, -1:], rows, sides[:, :, :1]], axis=2).astype(jnp.bfloat16)
    padded = jnp.pad(padded, ((0, 0), (1, 1), (0, 0)))
    padded = lax.dynamic_slice_in_dim(padded, guide_at * half_rows, half_rows + 2, 1)
    features = convolve(padded, w_dec)
    return (denoised, features)


def solution(mesh):
    return jax.shard_map(
        shards,
        mesh=mesh,
        in_specs=(
            P(None, None, ("groups", "width")),
            P(("groups", "width")),
            P(("groups", "width")),
            P("groups"),
            P("guide", None, None),
            P(),
            P("width", None),
            P(),
            P(),
            P(),
        ),
        out_specs=(P(None, "guide", ("groups", "width")), P("guide", ("groups", "width"), None)),
        check_vma=False,
    )
```

```python
import functools
import math

import jax
import jax.numpy as jnp
from jax import lax
from jax.experimental import pallas as pl
from jax.experimental.pallas import tpu as pltpu
from jax.sharding import PartitionSpec as P

HEAD = 64
STEPS = 28
LANES = 128
MESH = pl.DeviceIdType.MESH

guidance = 4.0
epsilon = 1e-06


def at(groups, width):
    return {"groups": groups, "width": width}


def column_map(shape, column_dim, parity, offset):
    column = lax.broadcasted_iota(jnp.int32, shape, column_dim)
    patch = lax.broadcasted_iota(jnp.int32, shape, 1 - column_dim)
    hit = column == 2 * patch + (parity + offset)
    return jnp.where(hit, 1.0, 0.0).astype(jnp.bfloat16)


def dot(a, b):
    return jnp.dot(a, b, preferred_element_type=jnp.float32)


def row_map(shape, natural_dim, channels, height):
    natural = lax.broadcasted_iota(jnp.int32, shape, natural_dim)
    moved = lax.broadcasted_iota(jnp.int32, shape, 1 - natural_dim)
    hit = natural == lax.rem(moved, channels) * height + moved // channels
    return jnp.where(hit, 1.0, 0.0).astype(jnp.bfloat16)


def fold_rows(modulation, w_patch, depth, w):
    patch = w_patch[...].astype(jnp.float32)
    patch = patch - jnp.mean(patch, axis=1, keepdims=True)
    shift = jnp.broadcast_to(modulation[0], (16, patch.shape[1]))
    rows = jnp.concatenate([patch * (1.0 + modulation[1]), shift], axis=0)
    total = rows.shape[1]
    rows = pltpu.roll(rows, lax.rem(total - w * depth, total), 1)[:, :depth]
    high = rows.astype(jnp.bfloat16)
    return high, (rows - high.astype(jnp.float32)).astype(jnp.bfloat16)


def step_kernel(
    groups, n,
    starts, step_index, latent, counts, mod, w_patch, w_final, w_dec, w_qkv_hbm, w_out_hbm,
    clean, feats,
    w_qkv, w_out, high, low, soft, edges, softs, edge_pair, parts, arrived, full, shifts,
    pat, rstd, att, turned_v, v, other, outgoing, incoming, taps,
    load_sem, send_a, recv_a, send_c, send_b, recv_b, send_x, recv_x, send_v, recv_v, send, recv,
):
    g = lax.axis_index("groups")
    w = lax.axis_index("width")
    e = lax.axis_index("guide")
    owners = groups * n
    me = g * n + w
    features, size = full.shape[1:]
    area, columns = latent.shape
    channels = features // 4
    height = area // channels
    band = 2 * channels
    pieces = w_qkv.shape[1] // size
    barrier = pltpu.get_barrier_semaphore()

    @pl.loop(1, owners)
    def _(step):
        to = lax.rem(me + step, owners)
        pl.semaphore_signal(
            barrier, inc=1, device_id=at(to // n, lax.rem(to, n)), device_id_type=MESH
        )

    pl.semaphore_signal(barrier, inc=1, device_id={"guide": 1 - e}, device_id_type=MESH)
    load_qkv = pltpu.make_async_copy(w_qkv_hbm, w_qkv, load_sem.at[0])
    load_out = pltpu.make_async_copy(w_out_hbm, w_out, load_sem.at[1])
    load_qkv.start()
    load_out.start()

    own = latent[...]
    soft[...] = own.astype(jnp.bfloat16)
    turned = own.T
    index = jnp.full((1, columns), step_index[0], jnp.int32).astype(jnp.float32)
    fraction = (index + 1.0) / STEPS
    sigma = 3.0 * fraction / (1.0 + 2.0 * fraction)
    cover = counts[...].astype(jnp.float32)
    edges[...] = jnp.concatenate(
        [turned[:1], turned[columns - 1 :], cover, jnp.zeros((5, columns), jnp.float32)], axis=0
    )
    high_rows, low_rows = fold_rows(mod, w_patch, w_qkv.shape[0], w)
    high[...] = high_rows
    low[...] = low_rows
    load_qkv.wait()

    @pl.loop(0, n)
    def _(step):
        chunk = jnp.minimum(g * n + lax.rem(w + step, n), pieces - 1)
        cut = w_qkv[:, pl.ds(pl.multiple_of(chunk * size, LANES), size)]
        parts[step] = (dot(high[:features], cut) + dot(low[:features], cut)).astype(jnp.bfloat16)

    @pl.when(g == pieces // n)
    def _():
        line = dot(high[features:], w_qkv[...]) + dot(low[features:], w_qkv[...])
        lines = jnp.concatenate([line[:1, i * size : (i + 1) * size] for i in range(pieces)], axis=0)
        lines = jnp.concatenate(
            [lines, jnp.zeros((features - pieces, size), jnp.float32)], axis=0
        )
        parts[lax.rem(pieces % n - w + n, n)] = lines.astype(jnp.bfloat16)

    pl.semaphore_wait(barrier, owners)

    def remote(source, target, sent, received, shift):
        return pltpu.make_async_remote_copy(
            src_ref=source, dst_ref=target, send_sem=sent, recv_sem=received,
            device_id=at(g, lax.rem(w + shift + n, n)), device_id_type=MESH,
        )

    def scatter(step):
        return remote(parts.at[step], arrived.at[step], send_a.at[step], recv_a.at[step], step)

    @pl.loop(1, n)
    def _(step):
        scatter(step).start()

    moves = [
        remote(soft, softs.at[0], send_x.at[0], recv_x.at[0], -1),
        remote(soft, softs.at[1], send_x.at[1], recv_x.at[1], -2),
        remote(edges, edge_pair.at[0], send_x.at[2], recv_x.at[2], -1),
        remote(edges, edge_pair.at[1], send_x.at[3], recv_x.at[3], 1),
    ]
    for move in moves:
        move.start()

    @pl.loop(1, n)
    def _(step):
        scatter(step).wait_recv()

    def add(step, total):
        return total + arrived[step].astype(jnp.float32)

    full[me] = lax.fori_loop(1, n, add, parts[0].astype(jnp.float32)).astype(jnp.bfloat16)

    deep = n // 2
    sides = 2 * groups
    side = g * 2 + lax.rem(w, 2)
    level = w // 2

    def owner_of(which_side, which_level):
        return (which_side // 2) * n + which_level * 2 + lax.rem(which_side, 2)

    def passed(source, peer, sent):
        return pltpu.make_async_remote_copy(
            src_ref=full.at[source], dst_ref=full.at[source], send_sem=sent, recv_sem=recv_b.at[source],
            device_id=at(peer // n, lax.rem(peer, n)), device_id_type=MESH,
        )

    def along(step):
        return passed(me, owner_of(side, lax.rem(level + step, deep)), send_c.at[step])

    def aside(step, turn):
        source = owner_of(side, lax.rem(level + step, deep))
        peer = owner_of(lax.rem(side + turn, sides), level)
        return passed(source, peer, send_b.at[step, turn])

    @pl.loop(1, deep)
    def _(step):
        along(step).start()

    @pl.loop(1, sides)
    def _(turn):
        aside(0, turn).start()

    for move in moves:
        move.wait()
    offset = starts[0] - w * columns
    wide = jnp.concatenate([soft[...], softs[0], softs[1]], axis=1)
    wide = dot(row_map((area, area), 1, channels, height), wide).astype(jnp.bfloat16)
    spread = [dot(wide, column_map((3 * columns, columns), 0, b, offset)) for b in range(2)]
    for p in range(area // band):
        block = jnp.concatenate(
            [
                spread[b][p * band + a * channels : p * band + (a + 1) * channels]
                for a in range(2)
                for b in range(2)
            ],
            axis=0,
        )
        pat[p * columns : (p + 1) * columns] = block.T.astype(jnp.bfloat16)

    @pl.loop(1, deep)
    def _(step):
        source = owner_of(side, lax.rem(level + step, deep))
        passed(source, source, send_c.at[step]).wait_recv()

        @pl.loop(1, sides)
        def _(turn):
            aside(step, turn).start()

    tokens = pat.shape[0]
    step_rows = 2 * columns
    for start in range(0, tokens, step_rows):
        rows = slice(start, start + step_rows)
        hidden = dot(pat[rows], w_patch[...])
        centered = hidden - jnp.mean(hidden, axis=1, keepdims=True)
        rstd[rows] = jnp.broadcast_to(
            lax.rsqrt(jnp.mean(centered * centered, axis=1, keepdims=True) + epsilon),
            (step_rows, rstd.shape[1]),
        )
    each = w_out.shape[0] // size
    row_head = lax.broadcasted_iota(jnp.int32, (size, size), 0) // HEAD
    col_head = lax.broadcasted_iota(jnp.int32, (size, size), 1) // HEAD
    same_head = jnp.where(row_head == col_head, 1.0 / HEAD, 0.0).astype(jnp.bfloat16)
    scale = math.log2(math.e) / math.sqrt(HEAD)
    ones = jnp.ones((tokens, HEAD), jnp.bfloat16)

    def await_piece(source):
        own_side = (source // n) * 2 + lax.rem(source, 2)

        @pl.when(own_side != side)
        def _():
            passed(source, source, send_c.at[0]).wait_recv()

    @pl.loop(pieces, owners)
    def _(source):
        await_piece(source)

    shifts[...] = full[pieces].astype(jnp.float32)

    def project(i):
        return dot(pat[...], full[i]) * rstd[:, :1] + shifts[pl.ds(i, 1)]

    def head_norm(values):
        square = dot((values * values).astype(jnp.bfloat16), same_head)
        return values * lax.rsqrt(square + epsilon)

    @pl.loop(0, each)
    def _(j):
        for i in range(3):
            await_piece(i * each + j)
        queries = (head_norm(project(j)) * scale).astype(jnp.bfloat16)
        keys = head_norm(project(each + j)).astype(jnp.bfloat16)
        values = project(2 * each + j).astype(jnp.bfloat16)
        mixed = []
        for h in range(size // HEAD):
            cut = slice(h * HEAD, (h + 1) * HEAD)
            scores = lax.dot_general(
                queries[:, cut], keys[:, cut], (((1,), (1,)), ((), ())),
                preferred_element_type=jnp.float32,
            )
            weights = jnp.exp2(scores).astype(jnp.bfloat16)
            sums = dot(weights, jnp.concatenate([values[:, cut], ones], axis=1))
            mixed.append(sums[:, :HEAD] / sums[:, HEAD:])
        att[:, pl.ds(pl.multiple_of(j * size, LANES), size)] = jnp.concatenate(mixed, axis=1).astype(
            jnp.bfloat16
        )

    load_out.wait()
    for start in range(0, tokens, step_rows):
        rows = slice(start, start + step_rows)
        residual = dot(pat[rows], w_patch[...]) + mod[2] * dot(att[rows], w_out[...])
        centered = residual - jnp.mean(residual, axis=1, keepdims=True)
        spread_of = jnp.mean(centered * centered, axis=1, keepdims=True)
        final_in = (centered * lax.rsqrt(spread_of + epsilon)).astype(jnp.bfloat16)
        found = lax.dot_general(
            final_in, w_final[...], (((1,), (1,)), ((), ())), preferred_element_type=jnp.float32
        )
        for i in range(step_rows // columns):
            p = start // columns + i
            turned = found[i * columns : (i + 1) * columns].T.astype(jnp.bfloat16)
            laid = [dot(turned, column_map((columns, 3 * columns), 1, b, offset)) for b in range(2)]
            for a in range(2):
                at_row = a * band
                turned_v[p * band + a * channels : p * band + (a + 1) * channels] = (
                    laid[0][at_row : at_row + channels] + laid[1][at_row + channels : at_row + band]
                ).astype(jnp.bfloat16)
    v[...] = dot(row_map((area, area), 0, channels, height), turned_v[...]).astype(jnp.bfloat16)

    swap = pltpu.make_async_remote_copy(
        src_ref=v, dst_ref=other, send_sem=send_v, recv_sem=recv_v,
        device_id={"guide": 1 - e}, device_id_type=MESH,
    )
    swap.start()
    swap.wait()
    mine = v[...].astype(jnp.float32)
    theirs = other[...].astype(jnp.float32)
    first = e == 0
    with_text = jnp.where(first, mine, theirs)
    plain = jnp.where(first, theirs, mine)
    guided = plain + guidance * (with_text - plain)
    here, ahead, further = (guided[:, i * columns : (i + 1) * columns] for i in range(3))
    at_end = lax.broadcasted_iota(jnp.int32, (area, columns), 1) == columns - 1
    outgoing[0] = ahead.astype(jnp.bfloat16)
    outgoing[1] = jnp.where(at_end, here, further).astype(jnp.bfloat16)
    outgoing[2] = jnp.where(at_end, ahead, further).astype(jnp.bfloat16)
    outgoing[3] = here.astype(jnp.bfloat16)
    moves = [
        remote(outgoing.at[i], incoming.at[i], send.at[i], recv.at[i], shift)
        for i, shift in enumerate((1, 1, 2, -1))
    ]
    for move in moves:
        move.start()

    @pl.loop(1, n)
    def _(step):
        scatter(step).wait_send()

    @pl.loop(1, deep)
    def _(step):
        along(step).wait_send()

    @pl.loop(0, deep)
    def _(step):
        @pl.loop(1, sides)
        def _(turn):
            aside(step, turn).wait_send()

    for move in moves:
        move.wait()
    got = [incoming[i].astype(jnp.float32) for i in range(4)]
    total = here + got[0] + jnp.where(at_end, 0.0, got[2])
    done = own - sigma * (total / cover)
    half = height // 2
    grid = done.reshape(channels, height, columns)
    clean[...] = jnp.where(first, grid[:, :half], grid[:, half:])
    around = jnp.where(at_end, got[1] + got[2], got[3] + ahead + got[1])
    row_end = lax.broadcasted_iota(jnp.int32, (1, columns), 1) == columns - 1
    right_edges, left_edges = edge_pair[0], edge_pair[1]
    covered = jnp.where(row_end, left_edges[2:3], right_edges[2:3])
    beside = jnp.where(at_end, left_edges.T[:, 1:2], right_edges.T[:, 0:1])
    left = jnp.where(w > 0, 1.0, 0.0)
    right = jnp.where(w < n - 1, 1.0, 0.0)
    border = jnp.where(at_end, left, right) * (beside - sigma * (around / covered))
    moved = row_map((area, area), 1, channels, height)
    center = dot(moved, done.astype(jnp.bfloat16))
    border = dot(moved, border.astype(jnp.bfloat16))
    at_start = lax.broadcasted_iota(jnp.int32, (area, columns), 1) == 0
    before = jnp.where(at_start, pltpu.roll(border, 1, 1), pltpu.roll(center, 1, 1))
    after = jnp.where(
        at_end, pltpu.roll(border, columns - 1, 1), pltpu.roll(center, columns - 1, 1)
    )
    empty = jnp.zeros((channels, columns), jnp.bfloat16)
    for b, tap in enumerate((before, center, after)):
        taps[b, :channels] = empty
        taps[b, channels : channels + area] = tap.astype(jnp.bfloat16)
        taps[b, channels + area :] = empty
    for i in range(half):
        cuts = []
        for a in range(3):
            row = pl.multiple_of((e * half + i + a) * channels, channels)
            cuts += [taps[b, pl.ds(row, channels)] for b in range(3)]
        stacked = jnp.concatenate(cuts, axis=0).astype(jnp.float32).T.astype(jnp.bfloat16)
        summed = dot(stacked, w_dec[...])
        feats[i] = (summed / (1.0 + jnp.exp(-summed))).astype(jnp.bfloat16)


def run_step(groups, n, starts, step_index, own, counts, mod, w_patch, w_final, w_dec, w_qkv, w_out):
    total = w_qkv.shape[1]
    owners = groups * n
    size = LANES * -(-total // (LANES * owners))
    while (total // 3) % size or total // size >= owners:
        size += LANES
    area, columns = own.shape
    features = w_patch.shape[0]
    channels = features // 4
    height = area // channels
    tokens = area * 2 * columns // features
    dma = pltpu.SemaphoreType.DMA
    vmem = pl.BlockSpec(memory_space=pltpu.VMEM)
    smem = pl.BlockSpec(memory_space=pltpu.SMEM)
    hbm = pl.BlockSpec(memory_space=pl.ANY)
    half, single = jnp.bfloat16, jnp.float32
    return pl.pallas_call(
        functools.partial(step_kernel, groups, n),
        name="guided_step",
        out_shape=(
            jax.ShapeDtypeStruct((channels, height // 2, columns), single),
            jax.ShapeDtypeStruct((height // 2, columns, w_dec.shape[1]), half),
        ),
        in_specs=[smem] * 2 + [vmem] * 6 + [hbm] * 2,
        out_specs=(vmem, vmem),
        scratch_shapes=[
            pltpu.VMEM(w_qkv.shape, half),
            pltpu.VMEM(w_out.shape, half),
            pltpu.VMEM((features + 16, w_qkv.shape[0]), half),
            pltpu.VMEM((features + 16, w_qkv.shape[0]), half),
            pltpu.VMEM(own.shape, half),
            pltpu.VMEM((8, columns), single),
            pltpu.VMEM((2, *own.shape), half),
            pltpu.VMEM((2, 8, columns), single),
            pltpu.VMEM((n, features, size), half),
            pltpu.VMEM((n, features, size), half),
            pltpu.VMEM((owners, features, size), half),
            pltpu.VMEM((features, size), single),
            pltpu.VMEM((tokens, features), half),
            pltpu.VMEM((tokens, LANES), single),
            pltpu.VMEM((tokens, w_out.shape[0]), half),
            pltpu.VMEM((area, 3 * columns), half),
            pltpu.VMEM((area, 3 * columns), half),
            pltpu.VMEM((area, 3 * columns), half),
            pltpu.VMEM((4, *own.shape), half),
            pltpu.VMEM((4, *own.shape), half),
            pltpu.VMEM((3, area + 2 * channels, columns), half),
            dma((2,)), dma((n,)), dma((n,)), dma((n // 2,)), dma((n // 2, 2 * groups)), dma((owners,)), dma((4,)), dma((4,)),
            dma, dma, dma((4,)), dma((4,)),
        ],
        compiler_params=pltpu.CompilerParams(
            collective_id=0, has_side_effects=True, vmem_limit_bytes=56 << 20
        ),
    )(starts, step_index, own, counts, mod, w_patch, w_final, w_dec, w_qkv, w_out)


def shards(latent, starts, counts, step_index, cond_mod, w_patch, w_qkv, w_out, w_final, w_dec):
    groups, n = lax.axis_size("groups"), lax.axis_size("width")
    channels, height, columns = latent.shape
    own = latent.reshape(channels * height, columns)
    return run_step(
        groups, n, starts, step_index, own, counts[None], cond_mod.transpose(1, 0, 2),
        w_patch, w_final.T, w_dec, w_qkv, w_out,
    )


def solution(mesh):
    return jax.shard_map(
        shards,
        mesh=mesh,
        in_specs=(
            P(None, None, ("groups", "width")),
            P(("groups", "width")),
            P(("groups", "width")),
            P("groups"),
            P("guide", None, None),
            P(),
            P("width", None),
            P(),
            P(),
            P(),
        ),
        out_specs=(P(None, "guide", ("groups", "width")), P("guide", ("groups", "width"), None)),
        check_vma=False,
    )
```
